32 devices in a mesh: channel: 4 (over z), left: 2 (over y), right: 4 (over x, core).
Axes of the slice: x: 2, y: 2, z: 4, core: 2. Of those that a mesh axis runs over, the one named last changes fastest.
Arguments:
- state: float32 [4, 1024, 1024], P(None, 'left', 'right'), may hold values from -6 to 6
- left_env: float32 [16, 1024, 1024], P('channel', 'left', 'right'), may hold values from -0.5 to 0.5
- right_env: float32 [16, 1024, 1024], P('channel', None, ('left', 'right')), may hold values from -0.5 to 0.5
- left_sizes: int32 [8], replicated, may hold values from 1 to 512, 1024 in all
- right_sizes: int32 [8], replicated, may hold values from 1 to 512, 1024 in all
- left_blocks: int32 [16, 8], replicated, may hold values from 0 to 7
- right_blocks: int32 [16, 8], replicated, may hold values from 0 to 7
- couple_to: int32 [16, 2], replicated, may hold values from 0 to 15
- couple_coef: int32 [16, 2], replicated, may hold values from 0 to 3
- coefs: float32 [4, 4, 4], replicated, may hold values from -4 to 4
Outputs:
- applied: float32 [4, 1024, 1024], P(None, ('left', 'right'), 'channel')
The draws below stay inside these ranges and needn't reach their ends.
Inputs may be any that keep to these rules, and one draw needn't show every extreme that they name: `left_sizes`: they sum to 1024, and the largest is half of 1024. `right_sizes`: they sum to 1024, and the largest is half of 1024. `couple_to`: a right channel may be named several times or not at all.
All inputs are finite; a program needn't handle non-finite values.
Results may differ from the reference program's by a relative error of at most 0.000071.
Values sent between devices are 32-bit elements; how exact they have to be, the bound alone decides.
No kernel may reach another device: no remote copies, remote signals or barrier semaphores. Data moves between devices by JAX's collectives and lax.ppermute only.
A program may use at most 128 MiB of HBM per device.

```python
import math
import jax
import jax.numpy as jnp
import numpy as np
from jax import lax

K = 16
P_SIZE = 4
NSEC = 8
NCOEF = 4
KC = 2
ML = 1024
MR = 1024


def set_ends(entries, stream_key, least, high):
    shape = entries.shape
    spot = [jax.random.randint(jax.random.fold_in(stream_key, axis), (), 0, shape[axis]) for axis in range(len(shape))]
    entries = entries.at[tuple(spot)].set(least)
    longest = shape.index(max(shape))
    spot[longest] = (spot[longest] + 1) % shape[longest]
    return entries.at[tuple(spot)].set(high)


def shard_levels(key, dims, pieces, smallest, largest):
    level, own = 1.0, jax.random.fold_in(key, 6)
    for axis_at, blocks in pieces:
        steps = jnp.exp(jax.random.uniform(jax.random.fold_in(own, axis_at), (blocks,), jnp.float32, smallest / len(pieces), largest / len(pieces)))
        level = level * jnp.repeat(steps, dims[axis_at] // blocks).reshape([-1 if axis == axis_at else 1 for axis in range(len(dims))])
    return level


def length_profile(number_of, total, most, lean):
    loads = [(1 << 20) // math.isqrt(rank ** lean) + 1 for rank in range(2, number_of + 1)]
    rest, holding = total - most - (number_of - 1), [1] * (number_of - 1)
    while rest > 0:
        free = [i for i in range(number_of - 1) if holding[i] < most]
        pool, remaining = sum([loads[i] for i in free]), rest
        for i in free:
            more = min(most - holding[i], max(1, remaining * loads[i] // pool), rest)
            holding[i] = holding[i] + more
            rest = rest - more
    return np.array([most] + holding)


def ragged_sizes(stream_key, count, total, bound, slope):
    if count == 2:
        one = jax.random.randint(stream_key, (), max(1, total - bound), min(bound, total - 1) + 1)
        return jnp.stack([one, total - one])
    lengths = jnp.asarray(length_profile(count, total, bound, slope), jnp.int32)
    twos = (count - 1) // 2
    donor, sink = lengths[1:1 + 2 * twos:2], lengths[2:2 + 2 * twos:2]
    slack = jnp.minimum(donor - 1, bound - sink)
    passed = jax.random.randint(jax.random.fold_in(stream_key, 1), (twos,), 0, 1 << 20) % (slack + 1)
    lengths = lengths.at[1:1 + 2 * twos:2].set(donor - passed).at[2:2 + 2 * twos:2].set(sink + passed)
    return lengths[jax.random.permutation(jax.random.fold_in(stream_key, 2), count)]


def normal_values(own_key, dims, deviation, bound, shards=(), kind=jnp.bfloat16):
    drawn = deviation * jax.random.normal(own_key, dims, jnp.float32)
    if shards:
        drawn = drawn * shard_levels(own_key, dims, shards, -0.22, 0.18)
    return jnp.clip(drawn, -bound, bound).astype(kind)


def setup_inputs(seed: int = 0) -> dict:
    arg_keys = jax.random.split(jax.random.key(seed), 11)
    return {
        "state": normal_values(arg_keys[0], (P_SIZE, ML, MR), 1.0, 6.0, ((1, 2), (2, 4)), jnp.float32),
        "left_env": normal_values(arg_keys[1], (K, ML, ML), (ML // NSEC) ** -0.5, 0.5, ((0, 4), (1, 2), (2, 4)), jnp.float32),
        "right_env": normal_values(arg_keys[2], (K, MR, MR), (MR // NSEC) ** -0.5, 0.5, ((0, 4), (2, 8)), jnp.float32),
        "left_sizes": ragged_sizes(arg_keys[3], NSEC, ML, ML // 2, 1).astype(jnp.int32),
        "right_sizes": ragged_sizes(arg_keys[4], NSEC, MR, MR // 2, 1).astype(jnp.int32),
        "left_blocks": set_ends(jax.random.randint(arg_keys[5], (K, NSEC), 0, NSEC), jax.random.fold_in(arg_keys[5], 1), 0, NSEC - 1).astype(jnp.int32),
        "right_blocks": set_ends(jax.random.randint(arg_keys[6], (K, NSEC), 0, NSEC), jax.random.fold_in(arg_keys[6], 1), 0, NSEC - 1).astype(jnp.int32),
        "couple_to": set_ends(jax.random.randint(arg_keys[7], (K, KC), 0, K), jax.random.fold_in(arg_keys[7], 1), 0, K - 1).astype(jnp.int32),
        "couple_coef": set_ends(jax.random.randint(arg_keys[8], (K, KC), 0, NCOEF), jax.random.fold_in(arg_keys[8], 1), 0, NCOEF - 1).astype(jnp.int32),
        "coefs": normal_values(arg_keys[9], (NCOEF, P_SIZE, P_SIZE), 0.7, 4.0, (), jnp.float32),
    }


def sector_ids(sizes, count):
    bounds = jnp.cumsum(sizes).astype(jnp.int32)
    places = jnp.arange(count, dtype=jnp.int32)
    return jnp.sum((places[:, None] >= bounds[None, :-1]).astype(jnp.int32), axis=1)


def block_targets(blocks, ids):
    sectors = blocks.shape[1]
    onehot = (ids[:, None] == jnp.arange(sectors, dtype=jnp.int32)[None, :]).astype(jnp.int32)
    return jnp.sum(onehot[None, :, :] * blocks[:, None, :], axis=2)


def mixing_table(couple_to, couple_coef, coefs):
    channels = couple_to.shape[0]
    kinds = coefs.shape[0]
    partner = (couple_to[:, :, None] == jnp.arange(channels, dtype=jnp.int32)[None, None, :]).astype(jnp.float32)
    chosen = (couple_coef[:, :, None] == jnp.arange(kinds, dtype=jnp.int32)[None, None, :]).astype(jnp.float32)
    physical = jnp.einsum('kcn,nst->kcst', chosen, coefs, precision=lax.Precision.HIGHEST)
    return jnp.einsum('kcj,kcst->jskt', partner, physical, precision=lax.Precision.HIGHEST)


def reference(state, left_env, right_env, left_sizes, right_sizes, left_blocks, right_blocks, couple_to, couple_coef, coefs):
    left_ids = sector_ids(left_sizes, ML)
    right_ids = sector_ids(right_sizes, MR)
    left_target = block_targets(left_blocks, left_ids)
    right_target = block_targets(right_blocks, right_ids)
    left_masked = jnp.where(left_ids[None, None, :] == left_target[:, :, None], left_env, 0.0)
    right_masked = jnp.where(right_ids[None, None, :] == right_target[:, :, None], right_env, 0.0)
    products = jnp.einsum('kab,sbc->ksac', left_masked, state, precision=lax.Precision.HIGHEST)
    table = mixing_table(couple_to, couple_coef, coefs)
    mixed = jnp.einsum('jskt,ktac->jsac', table, products, precision=lax.Precision.HIGHEST)
    return jnp.einsum('jsac,jcd->sad', mixed, right_masked, precision=lax.Precision.HIGHEST)
```

```python
import functools

import jax
import jax.numpy as jnp
from jax import lax
from jax.experimental import pallas as pl
from jax.experimental.pallas import tpu as pltpu
from jax.sharding import PartitionSpec as P


def sector_ids(sizes, first, count):
    bounds = jnp.cumsum(sizes)
    places = first + jnp.arange(count, dtype=jnp.int32)
    return jnp.sum((places[:, None] >= bounds[None, :-1]).astype(jnp.int32), axis=1)


def block_targets(blocks, ids):
    sectors = blocks.shape[1]
    onehot = (ids[:, None] == jnp.arange(sectors, dtype=jnp.int32)[None, :]).astype(jnp.int32)
    return jnp.sum(onehot[None, :, :] * blocks[:, None, :], axis=2)


def mixing_table(couple_to, couple_coef, coefs):
    channels = couple_to.shape[0]
    kinds = coefs.shape[0]
    partner = (
        couple_to[:, :, None] == jnp.arange(channels, dtype=jnp.int32)[None, None, :]
    ).astype(jnp.float32)
    chosen = (couple_coef[:, :, None] == jnp.arange(kinds, dtype=jnp.int32)[None, None, :]).astype(
        jnp.float32
    )
    physical = jnp.einsum("kcn,nst->kcst", chosen, coefs, precision=lax.Precision.HIGHEST)
    return jnp.einsum("kcj,kcst->jskt", partner, physical, precision=lax.Precision.HIGHEST)


def gathered_body(
    state,
    left_env,
    right_env,
    left_sizes,
    right_sizes,
    left_blocks,
    right_blocks,
    couple_to,
    couple_coef,
    coefs,
):
    local_channels = left_env.shape[0]
    row_count = left_env.shape[1]
    first_channel = lax.axis_index("channel") * local_channels
    own_left = lax.dynamic_slice_in_dim(left_blocks, first_channel, local_channels, 0)
    own_right = lax.dynamic_slice_in_dim(right_blocks, first_channel, local_channels, 0)
    row_ids = sector_ids(left_sizes, lax.axis_index("left") * row_count, row_count)
    row_target = block_targets(own_left, row_ids)
    columns = lax.all_gather(state, "left", axis=1, tiled=True)
    piece = lax.all_gather(left_env, "right", axis=2, tiled=True)
    breadth = piece.shape[2]
    column_ids = sector_ids(left_sizes, jnp.int32(0), breadth)
    masked = jnp.where(column_ids[None, None, :] == row_target[:, :, None], piece, 0.0)
    products = jnp.einsum("kab,sbc->ksac", masked, columns, precision=lax.Precision.HIGHEST)
    table = mixing_table(couple_to, couple_coef, coefs)
    regrouped = lax.all_to_all(products, "right", split_axis=2, concat_axis=3, tiled=True)
    everyone = lax.all_gather(regrouped, "channel", axis=0, tiled=True)
    owner_table = lax.dynamic_slice_in_dim(table, first_channel, local_channels, 0)
    mixed = jnp.einsum("jskt,ktac->jsac", owner_table, everyone, precision=lax.Precision.HIGHEST)
    right_ids = sector_ids(right_sizes, 0, right_env.shape[1])
    right_target = block_targets(own_right, right_ids)
    piece = lax.all_gather(right_env, ("left", "right"), axis=2, tiled=True)
    column_ids = sector_ids(right_sizes, jnp.int32(0), piece.shape[2])
    masked = jnp.where(column_ids[None, None, :] == right_target[:, :, None], piece, 0.0)
    partial_sum = jnp.einsum("jsac,jcd->sad", mixed, masked, precision=lax.Precision.HIGHEST)
    return lax.psum_scatter(partial_sum, "channel", scatter_dimension=2, tiled=True)


def split(x):
    high = x.astype(jnp.bfloat16)
    return high, (x - high.astype(jnp.float32)).astype(jnp.bfloat16)


def dot3(a_high, a_low, b_high, b_low):
    dot = functools.partial(jnp.dot, preferred_element_type=jnp.float32)
    return dot(a_high, b_high) + dot(a_high, b_low) + dot(a_low, b_high)


def products_kernel(count, scalars, *refs):
    lefts, targets = refs[:count], refs[count : 2 * count]
    ids, *pieces = refs[2 * count : -6]
    out, l_high, l_low, s_high, s_low = refs[-5:]
    pieces = pieces[:4]
    s, i = pl.program_id(0), pl.program_id(1)

    @pl.when(i == 0)
    def _():
        for n, piece in enumerate(pieces):
            rows = piece.shape[1]
            place = pl.ds(pl.multiple_of(scalars[2 * count + n], rows), rows)
            s_high[place, :], s_low[place, :] = split(piece[0])

    for n in range(count):

        @pl.when((i == n) & (s == 0))
        def _(n=n):
            half = lefts[n].shape[1]
            for x in range(2):
                columns = slice(x * half, (x + 1) * half)
                full = jnp.where(ids[:, columns] == targets[n][...], lefts[n][...], 0.0)
                l_high[n, :, columns], l_low[n, :, columns] = split(full)

    @pl.when(scalars[i] == 1)
    def _():
        found = dot3(l_high[i], l_low[i], s_high[...], s_low[...])
        out[...] = found.reshape(out.shape)


def products_call(scalars, lefts, targets, ids, pieces, products, channels, slots):
    count = len(lefts)
    depth, half = lefts[0].shape
    rows = depth // channels
    states, part, width = pieces[0].shape
    whole = lambda shape: pl.BlockSpec(shape, lambda s, i, c: (0,) * len(shape))
    return pl.pallas_call(
        functools.partial(products_kernel, count),
        out_shape=jax.ShapeDtypeStruct((slots, states, rows, width), jnp.float32),
        grid_spec=pltpu.PrefetchScalarGridSpec(
            num_scalar_prefetch=1,
            grid=(states, count),
            in_specs=[whole((depth, half))] * count
            + [whole((depth, 1))] * count
            + [whole(ids.shape)]
            + [pl.BlockSpec((1, part, width), lambda s, i, c: (s, 0, 0))] * 4
            + [pl.BlockSpec(memory_space=pl.ANY)],
            out_specs=pl.BlockSpec(
                (channels, 1, rows, width), lambda s, i, c: (c[count + i], s, 0, 0)
            ),
            scratch_shapes=[pltpu.VMEM((count, depth, 2 * half), jnp.bfloat16)] * 2
            + [pltpu.VMEM((4 * part, width), jnp.bfloat16)] * 2,
        ),
        input_output_aliases={1 + 2 * count + 1 + 4: 0},
        cost_estimate=pl.CostEstimate(
            flops=count * 6 * depth * 2 * half * states * width,
            bytes_accessed=count * 4 * depth * (half + states * width),
            transcendentals=0,
        ),
    )(scalars, *lefts, *targets, ids, *pieces, products)


def result_kernel(scalars, *refs):
    coefs, products = refs[:2]
    first, second = refs[2:4], refs[4:6]
    targets, ids, out = refs[6:9]
    mixed, m_high, m_low, r_high, r_low = refs[9:]
    step, steps = pl.program_id(0), pl.num_programs(0)
    states, rows, width = mixed.shape
    per, base = scalars[4], 6
    j = (step // per ^ scalars[0]) * per + step % per
    mixed[...] = jnp.zeros_like(mixed)
    piece_rows = min(rows, 16)

    def couple(e, _):
        k, n = scalars[base + steps + 1 + e], scalars[base + steps + 1 + scalars[5] + e]
        for r in range(0, rows, piece_rows):
            part = slice(r, r + piece_rows)
            found = [products[k, t, part, :] for t in range(states)]
            for s in range(states):
                total = mixed[s, part, :]
                for t in range(states):
                    total += coefs[(n * states + s) * states + t] * found[t]
                mixed[s, part, :] = total
        return 0

    lax.fori_loop(scalars[base + j], scalars[base + j + 1], couple, 0)
    for s in range(states):
        part = slice(s * rows, (s + 1) * rows)
        m_high[part, :], m_low[part, :] = split(mixed[s])

    columns = out.shape[0] * width
    tall, wide = first[0].shape[2:]

    def place(pair, chip_bit, left_bit):
        for n in range(8):
            piece = pair[n // 4][n % 4, 0]
            left = (n >> left_bit & 1) ^ scalars[2]
            chip = (n >> chip_bit & 1) ^ scalars[3]
            core = (n >> 2) ^ scalars[1]
            down = pl.ds(pl.multiple_of(left * tall, tall), tall)
            for h in range(2):
                start = h * (columns // 2) + (chip * 2 + core) * wide
                across = pl.ds(pl.multiple_of(start, wide), wide)
                kept = jnp.where(ids[:, across] == targets[0, down, :], piece, 0.0)
                r_high[down, across], r_low[down, across] = split(kept)

    @pl.when(step < steps // 2)
    def _():
        place(first, 1, 0)

    @pl.when(step >= steps // 2)
    def _():
        place(second, 0, 1)

    planes = out.shape[0]
    for n in range(planes):
        start = lax.rem(scalars[0] + n, planes) * width
        across = pl.ds(pl.multiple_of(start, width), width)
        found = dot3(m_high[...], m_low[...], r_high[:, across], r_low[:, across])
        found = found.reshape(out.shape[1:])

        @pl.when(step == 0)
        def _():
            out[n] = found

        @pl.when(step > 0)
        def _():
            out[n] += found


def result_call(scalars, coefs, products, first, second, targets, ids, planes):
    steps, depth, _ = targets.shape
    _, states, rows, width = products.shape
    _, count, tall, wide = first[0].shape
    flops = 6 * steps * states * rows * depth * planes * width
    return pl.pallas_call(
        result_kernel,
        out_shape=jax.ShapeDtypeStruct((planes, states, rows, width), jnp.float32),
        grid_spec=pltpu.PrefetchScalarGridSpec(
            num_scalar_prefetch=1,
            grid=(steps,),
            in_specs=[
                pl.BlockSpec(memory_space=pltpu.SMEM),
                pl.BlockSpec(
                    products.shape, lambda i, c: (0, 0, 0, 0), pipeline_mode=pl.Buffered(1)
                ),
            ]
            + [pl.BlockSpec((4, 1, tall, wide), lambda i, c: (0, jnp.minimum(i, count - 1), 0, 0))] * 2
            + [pl.BlockSpec((4, 1, tall, wide), lambda i, c: (0, jnp.maximum(i - count, 0), 0, 0))] * 2
            + [
                pl.BlockSpec((1, depth, 1), lambda i, c: (i, 0, 0)),
                pl.BlockSpec(ids.shape, lambda i, c: (0, 0)),
            ],
            out_specs=pl.BlockSpec((planes, states, rows, width), lambda i, c: (0, 0, 0, 0)),
            scratch_shapes=[
                pltpu.VMEM((states, rows, width), jnp.float32),
                pltpu.VMEM((states * rows, depth), jnp.bfloat16),
                pltpu.VMEM((states * rows, depth), jnp.bfloat16),
                pltpu.VMEM((depth, planes * width), jnp.bfloat16),
                pltpu.VMEM((depth, planes * width), jnp.bfloat16),
            ],
        ),
        cost_estimate=pl.CostEstimate(flops=flops, bytes_accessed=1 << 24, transcendentals=0),
    )(scalars, coefs, products, *first, *second, targets, ids)


def swap(x, axis, bit):
    size = lax.axis_size(axis)
    return lax.ppermute(x, axis, [(i, i ^ bit) for i in range(size)])


def pick(x, axis, index, count=1):
    return lax.dynamic_slice_in_dim(x, index * count, count, axis)


def gather_state(state, z, y, r, core):
    nz, nr = lax.axis_size("channel"), lax.axis_size("right")
    part = state.shape[1] // 2
    axes = ("channel", "right")
    sent = pick(state, 1, 1 - core, part)
    held = pick(state, 1, core, part)
    got = lax.ppermute(sent, axes, [(i * nr + i, i * nr + (i ^ 1)) for i in range(nz)])
    held = jnp.where(r == z, held, got)
    owners = {i: {i, i ^ 1} for i in range(nz)}
    bit = 2
    while bit < nr:
        pairs = [(i * nr + o, i * nr + (o ^ bit)) for i in range(nz) for o in sorted(owners[i])]
        got = lax.ppermute(held, axes, pairs)
        distance = r ^ z
        held = jnp.where(distance < bit, held, got)
        owners = {i: owners[i] | {o ^ bit for o in owners[i]} for i in range(nz)}
        bit *= 2
    far = swap(held, "left", 1)
    near_half, far_half = swap(held, "right", 1), swap(far, "right", 1)
    return held, near_half, far, far_half


def fold_left(left_env, target, z, y, r):
    channels, rows, width = left_env.shape
    nr = lax.axis_size("right")
    ids = target[1]
    masked = jnp.where(ids[None, None, :] == target[0][:, :, None], left_env, 0.0)
    masked = masked.reshape(channels, nr, rows // nr, width)
    got = [pick(masked, 1, r)[:, 0]]
    for bit in range(1, nr):
        got.append(swap(pick(masked, 1, r ^ bit)[:, 0], "right", bit))
    folded = [got[n] + got[n ^ (nr // 2)] for n in range(nr // 2)]
    own = r % (nr // 2)
    even = jnp.where(own == 0, folded[0], folded[1])
    odd = jnp.where(own == 0, folded[1], folded[0])
    return jnp.concatenate([even, odd], axis=2).reshape(channels * rows // nr, 2 * width)


def fold_right(right_env, target, z, y):
    channels, rows, width = right_env.shape
    nz = lax.axis_size("channel")
    masked = jnp.where(target[1][None, None, :] == target[0][:, :, None], right_env, 0.0)
    masked = masked.reshape(channels, nz, 2, rows // nz // 2, width)
    folded = pick(masked, 2, y)[:, :, 0] + swap(pick(masked, 2, 1 - y)[:, :, 0], "left", 1)
    planes = [pick(folded, 1, z)[:, 0]]
    for bit in range(1, nz):
        planes.append(swap(pick(folded, 1, z ^ bit)[:, 0], "channel", bit))
    return planes


def gather_plane(mine, order):
    for axis, bit in order:
        mine = jnp.concatenate([mine, swap(mine, axis, bit)], axis=0)
    return mine, swap(mine, "right", 1)


def folded_body(
    state,
    left_env,
    right_env,
    left_sizes,
    right_sizes,
    left_blocks,
    right_blocks,
    couple_to,
    couple_coef,
    coefs,
):
    nz, ny, nr = (lax.axis_size(a) for a in ("channel", "left", "right"))
    z, y, r = (lax.axis_index(a) for a in ("channel", "left", "right"))
    core, chip = r % 2, r // 2
    channels, span, left_width = left_env.shape
    bond, right_width = right_env.shape[1:]
    total = channels * nz
    rows, width = span // nr, bond // nz
    sectors = left_blocks.shape[1]

    own_left, own_right = pick(left_blocks, 0, z, channels), pick(right_blocks, 0, z, channels)
    left_target = block_targets(own_left, sector_ids(left_sizes, y * span, span))
    left_own = sector_ids(left_sizes, r * left_width, left_width)
    right_target = block_targets(own_right, sector_ids(right_sizes, 0, bond))
    right_own = sector_ids(right_sizes, (y * nr + r) * right_width, right_width)

    folded = fold_left(left_env, (left_target, left_own), z, y, r)
    planes = fold_right(right_env, (right_target, right_own), z, y)
    pieces = gather_state(state, z, y, r, core)

    row_ids = sector_ids(left_sizes, (y * nr + r) * rows, rows)
    row_target = block_targets(left_blocks, row_ids).reshape(nz, channels * rows)
    left_ids = sector_ids(left_sizes, 0, span * ny)[None, :]
    part = pieces[0].shape[1]
    places = [(a ^ y) * span + (b ^ core) * part for a in range(2) for b in range(2)]

    slots = total + channels
    products = jnp.zeros((slots, state.shape[0], rows, width), jnp.float32)

    def multiply(products, blocks, sources):
        valid = [((s >= 0) & (s < nz)).astype(jnp.int32) for s in sources]
        where = [jnp.where(v == 1, s, nz) for v, s in zip(valid, sources)]
        scalars = jnp.stack(valid + where + places).astype(jnp.int32)
        targets = [
            pick(row_target, 0, jnp.clip(s, 0, nz - 1)).reshape(channels * rows, 1) for s in sources
        ]
        return products_call(
            scalars, blocks, targets, left_ids, pieces, products, channels, slots
        )

    upward, downward = [folded], [folded]
    for t in range(1, nz):
        upward.append(
            lax.ppermute(upward[-1], "channel", [(i, i + 1) for i in range(t - 1, nz - 1)])
        )
        downward.append(
            lax.ppermute(downward[-1], "channel", [(i, i - 1) for i in range(1, nz - t + 1)])
        )
    products = multiply(products, [folded], [z])
    for t in range(1, nz):
        products = multiply(products, [upward[t], downward[t]], [z - t, z + t])

    near = jnp.concatenate(planes[: nz // 2], axis=0)
    far = jnp.concatenate(planes[nz // 2 :], axis=0)
    first = gather_plane(near[None], [("left", 1), ("right", 2)])
    second = gather_plane(far[None], [("right", 2), ("left", 1)])

    pairs = couple_to.size
    to, kind = couple_to.reshape(-1), couple_coef.reshape(-1)
    counter = jnp.arange(pairs, dtype=jnp.int32)
    before = (to[None, :] < to[:, None]) | (
        (to[None, :] == to[:, None]) & (counter[None, :] < counter[:, None])
    )
    rank = jnp.sum(before.astype(jnp.int32), axis=1)
    chosen = (rank[None, :] == counter[:, None]).astype(jnp.int32)
    source = jnp.sum(chosen * (counter // couple_to.shape[1])[None, :], axis=1)
    kinds = jnp.sum(chosen * kind[None, :], axis=1)
    marks = jnp.arange(total + 1, dtype=jnp.int32)
    bounds = jnp.sum((to[None, :] < marks[:, None]).astype(jnp.int32), axis=1)
    scalars = jnp.concatenate(
        [jnp.stack([z, core, y, chip, jnp.int32(channels), jnp.int32(pairs)]), bounds, source, kinds]
    ).astype(jnp.int32)

    turned = jnp.concatenate(
        [pick(right_blocks, 0, z ^ n, channels) for n in range(nz)], axis=0
    )
    column_target = block_targets(turned, sector_ids(right_sizes, z * width, width))
    right_ids = sector_ids(right_sizes, 0, bond)[None, :]
    parts = result_call(
        scalars,
        coefs.reshape(-1),
        products,
        first,
        second,
        column_target[:, :, None],
        right_ids,
        nz,
    )

    up = down = None
    for t in range(1, nz):
        up_part, down_part = parts[nz - t], parts[t]
        if t > 1:
            up_part, down_part = up_part + up, down_part + down
        up = lax.ppermute(up_part, "channel", [(i, i + 1) for i in range(t)])
        down = lax.ppermute(down_part, "channel", [(i, i - 1) for i in range(nz - t, nz)])
    return parts[0] + up + down


def whole_tiles(mesh, state_shape, left_shape, right_shape):
    nz, ny, nr = (mesh.shape[a] for a in ("channel", "left", "right"))
    bond = right_shape[1]
    return (
        nz == nr == 4
        and ny == 2
        and left_shape[0] % nz == 0
        and bond % (ny * nr * 128) == 0
        and left_shape[1] % (ny * nr * 128) == 0
    )


def solution(mesh):
    in_specs = (
        P(None, "left", "right"),
        P("channel", "left", "right"),
        P("channel", None, ("left", "right")),
        P(),
        P(),
        P(),
        P(),
        P(),
        P(),
        P(),
    )
    out_specs = P(None, ("left", "right"), "channel")

    def run(state, left_env, right_env, *tables):
        fits = whole_tiles(mesh, state.shape, left_env.shape, right_env.shape)
        chosen = folded_body if fits else gathered_body
        mapped = jax.shard_map(
            chosen, mesh=mesh, in_specs=in_specs, out_specs=out_specs, check_vma=False
        )
        return mapped(state, left_env, right_env, *tables)

    return run
```
